32 devices in a mesh: dp: 16 (over z, y, core), ctx: 2 (over x).
Axes of the slice: x: 2, y: 2, z: 4, core: 2. Of those that a mesh axis runs over, the one named last changes fastest.
Arguments:
- tokens: bfloat16 [32, 1024, 768], P('dp', 'ctx'), may hold values from -6 to 6
- out_grad: bfloat16 [32, 1024, 768], P('dp', 'ctx'), may hold values from -6 to 6
- logit_grad: float32 [32, 14], P('dp'), may hold values from -6 to 6
- piece_start: int32 [32, 2], P('dp'), may hold values from 0 to 960, as said below
- piece_len: int32 [32, 2], P('dp'), may hold values from 64 to 256, as said below
- qkv_weight: bfloat16 [768, 2304], P(('dp', 'ctx')), may hold values from -0.21875 to 0.21875
- query_bias: bfloat16 [768], P(('dp', 'ctx')), may hold values from -3 to 3
- value_bias: bfloat16 [768], P(('dp', 'ctx')), may hold values from -3 to 3
- out_weight: bfloat16 [768, 768], P(('dp', 'ctx')), may hold values from -0.875 to 0.875
- out_bias: bfloat16 [768], P(('dp', 'ctx')), may hold values from -3 to 3
- gain_one: bfloat16 [768], P(('dp', 'ctx')), may hold values from 0.5 to 1.5
- shift_one: bfloat16 [768], P(('dp', 'ctx')), may hold values from -3 to 3
- in_weight: bfloat16 [768, 3072], P(('dp', 'ctx')), may hold values from -0.21875 to 0.21875
- in_bias: bfloat16 [3072], P(('dp', 'ctx')), may hold values from -3 to 3
- back_weight: bfloat16 [3072, 768], P(('dp', 'ctx')), may hold values from -0.109375 to 0.109375
- back_bias: bfloat16 [768], P(('dp', 'ctx')), may hold values from -3 to 3
- gain_two: bfloat16 [768], P(('dp', 'ctx')), may hold values from 0.5 to 1.5
- shift_two: bfloat16 [768], P(('dp', 'ctx')), may hold values from -3 to 3
- reduce_weight: bfloat16 [768, 128], P(('dp', 'ctx')), may hold values from -0.21875 to 0.21875
- reduce_bias: bfloat16 [128], replicated, may hold values from -3 to 3
- pool_query: bfloat16 [128], replicated, may hold values from -16 to 16
- pool_weight: bfloat16 [128, 128], replicated, may hold values from -1 to 1
- pool_bias: bfloat16 [128], replicated, may hold values from -3 to 3
- class_weight: bfloat16 [128, 14], replicated, may hold values from -0.5 to 0.5
- class_bias: bfloat16 [14], replicated, may hold values from -6 to 6
Outputs:
- layer_out: bfloat16 [32, 1024, 768], P('dp', 'ctx')
- logits: float32 [32, 14], P('dp')
- token_grad: bfloat16 [32, 1024, 768], P('dp', 'ctx')
- qkv_weight_grad: float32 [768, 2304], P(('dp', 'ctx'))
- query_bias_grad: float32 [768], P(('dp', 'ctx'))
- value_bias_grad: float32 [768], P(('dp', 'ctx'))
- out_weight_grad: float32 [768, 768], P(('dp', 'ctx'))
- out_bias_grad: float32 [768], P(('dp', 'ctx'))
- gain_one_grad: float32 [768], P(('dp', 'ctx'))
- shift_one_grad: float32 [768], P(('dp', 'ctx'))
- in_weight_grad: float32 [768, 3072], P(('dp', 'ctx'))
- in_bias_grad: float32 [3072], P(('dp', 'ctx'))
- back_weight_grad: float32 [3072, 768], P(('dp', 'ctx'))
- back_bias_grad: float32 [768], P(('dp', 'ctx'))
- gain_two_grad: float32 [768], P(('dp', 'ctx'))
- shift_two_grad: float32 [768], P(('dp', 'ctx'))
- reduce_weight_grad: float32 [768, 128], P(('dp', 'ctx'))
- reduce_bias_grad: float32 [128], replicated
- pool_query_grad: float32 [128], replicated
- pool_weight_grad: float32 [128, 128], replicated
- pool_bias_grad: float32 [128], replicated
- class_weight_grad: float32 [128, 14], replicated
- class_bias_grad: float32 [14], replicated
The draws below stay inside these ranges and needn't reach their ends.
Inputs may be any that keep to these rules, and one draw needn't show every extreme that they name: `piece_len`: each sequence has 2 picture pieces; the first is exactly 256 tokens long. `piece_start`: piece k of a sequence lies wholly within positions k * 512 to (k + 1) * 512 - 1, so pieces never intersect.
All inputs are finite; a program needn't handle non-finite values.
Results may differ from the reference program's by a relative error of at most 0.017.
The reference program's roundings to bfloat16 on the way count: a program that leaves them out, or rounds other values in their place, can miss the bound.
Values may be sent and summed in bfloat16 or wider, within the bound.
No kernel may reach another device: no remote copies, remote signals or barrier semaphores. Data moves between devices by JAX's collectives and lax.ppermute only.
A program may use at most 256 MiB of HBM per device.

```python
import jax
import jax.numpy as jnp
from jax import lax

D = 768
H = 12
HD = 64
FF = 3072
RED = 128
PH = 2
CLS = 14
LEN = 1024
PIC = 256
NP = 2
SEQS = 32


def piece_table(key):
    size_key = jax.random.fold_in(key, 11)
    place_key = jax.random.fold_in(key, 12)
    region = LEN // NP
    column = jnp.arange(NP, dtype=jnp.int32)[None, :]
    lengths = jax.random.randint(size_key, (SEQS, NP), PIC // 4, PIC + 1)
    lengths = jnp.where(column == 0, PIC, lengths).astype(jnp.int32)
    offsets = jax.random.randint(place_key, (SEQS, NP), 0, region - lengths + 1)
    starts = column * region + offsets
    return (starts.astype(jnp.int32), lengths)


def draw_piece_start(key, part):
    return piece_table(key)[0]


def draw_piece_len(key, part):
    return piece_table(key)[1]


def levels(stream_key, shape, cuts, smallest, top_value):
    level = 1.0
    for position, parts in cuts:
        steps = jax.random.uniform(jax.random.fold_in(jax.random.fold_in(stream_key, 6), position), (parts,), jnp.float32, smallest / len(cuts), top_value / len(cuts))
        level = level * jnp.repeat(jnp.exp(steps), shape[position] // parts).reshape((-1,) + (1,) * (len(shape) - 1 - position))
    return level


def bell_draw(stream_key, shape, scale, most, split=(), kind=jnp.bfloat16):
    values = jax.random.normal(stream_key, shape, jnp.float32) * scale
    if len(split) > 0:
        values = levels(stream_key, shape, split, -0.22, 0.18) * values
    return jnp.clip(values, min=-most, max=most).astype(kind)


def setup_inputs(seed: int = 0) -> dict:
    key_of = jax.random.split(jax.random.key(seed), 26)
    tokens = bell_draw(key_of[0], (SEQS, LEN, D), 1.0, 6.0, ((0, 16), (1, 2)))
    out_grad = bell_draw(key_of[1], (SEQS, LEN, D), 1.0, 6.0, ((0, 16), (1, 2)))
    logit_grad = bell_draw(key_of[2], (SEQS, CLS), 1.0, 6.0, ((0, 16),), jnp.float32)
    piece_start = draw_piece_start(jax.random.fold_in(key_of[25], 71), 0)
    piece_len = draw_piece_len(jax.random.fold_in(key_of[25], 71), 0)
    qkv_weight = bell_draw(key_of[5], (D, 3 * D), D ** -0.5, 0.21875, ((0, 32),))
    query_bias = bell_draw(key_of[6], (D,), 0.5, 3.0, ((0, 32),))
    value_bias = bell_draw(key_of[7], (D,), 0.5, 3.0, ((0, 32),))
    out_weight = bell_draw(key_of[8], (D, D), (D // 16) ** -0.5, 0.875, ((0, 32),))
    out_bias = bell_draw(key_of[9], (D,), 0.5, 3.0, ((0, 32),))
    gain_one = jnp.clip(1.0 + 0.1 * jax.random.normal(key_of[10], (D,), jnp.float32), 0.5, 1.5).astype(jnp.bfloat16)
    shift_one = bell_draw(key_of[11], (D,), 0.5, 3.0, ((0, 32),))
    in_weight = bell_draw(key_of[12], (D, FF), D ** -0.5, 0.21875, ((0, 32),))
    in_bias = bell_draw(key_of[13], (FF,), 0.5, 3.0, ((0, 32),))
    back_weight = bell_draw(key_of[14], (FF, D), FF ** -0.5, 0.109375, ((0, 32),))
    back_bias = bell_draw(key_of[15], (D,), 0.5, 3.0, ((0, 32),))
    gain_two = jnp.clip(1.0 + 0.1 * jax.random.normal(key_of[16], (D,), jnp.float32), 0.5, 1.5).astype(jnp.bfloat16)
    shift_two = bell_draw(key_of[17], (D,), 0.5, 3.0, ((0, 32),))
    reduce_weight = bell_draw(key_of[18], (D, RED), D ** -0.5, 0.21875, ((0, 32),))
    reduce_bias = bell_draw(key_of[19], (RED,), 0.5, 3.0)
    pool_query = bell_draw(key_of[20], (RED,), 3.0, 16.0)
    pool_weight = bell_draw(key_of[21], (RED, RED), (RED // 4) ** -0.5, 1.0)
    pool_bias = bell_draw(key_of[22], (RED,), 0.5, 3.0)
    class_weight = bell_draw(key_of[23], (RED, CLS), RED ** -0.5, 0.5)
    class_bias = bell_draw(key_of[24], (CLS,), 1.0, 6.0)
    return dict(tokens=tokens, out_grad=out_grad, logit_grad=logit_grad, piece_start=piece_start, piece_len=piece_len, qkv_weight=qkv_weight, query_bias=query_bias, value_bias=value_bias, out_weight=out_weight, out_bias=out_bias, gain_one=gain_one, shift_one=shift_one, in_weight=in_weight, in_bias=in_bias, back_weight=back_weight, back_bias=back_bias, gain_two=gain_two, shift_two=shift_two, reduce_weight=reduce_weight, reduce_bias=reduce_bias, pool_query=pool_query, pool_weight=pool_weight, pool_bias=pool_bias, class_weight=class_weight, class_bias=class_bias)


@jax.custom_vjp
def low(v):
    return lax.optimization_barrier(v.astype(jnp.bfloat16)).astype(jnp.float32)

@jax.custom_vjp
def low_back(v):
    return v

def low_keep(v):
    return (low(v), None)

def low_pass(kept, grad):
    return (grad,)

def back_keep(v):
    return (v, None)

def back_low(kept, grad):
    return (low(grad),)
low.defvjp(low_keep, low_pass)
low_back.defvjp(back_keep, back_low)
negative = -1e+30
epsilon = 1e-06

def matmul(left, right):
    return jnp.matmul(left, right, precision=lax.Precision.HIGHEST)

def layer_norm(hidden, gain, shift):
    average = lax.optimization_barrier(jnp.mean(hidden, axis=-1, keepdims=True))
    centred = hidden - average
    variance = lax.optimization_barrier(jnp.mean(centred * centred, axis=-1, keepdims=True))
    return centred * lax.rsqrt(variance + epsilon) * gain + shift

def piece_labels(positions, starts, lengths):
    inside = (positions[:, None] >= starts[None, :]) & (positions[:, None] < (starts + lengths)[None, :])
    labels = jnp.arange(1, starts.shape[0] + 1, dtype=jnp.int32)
    return lax.optimization_barrier(jnp.sum(jnp.where(inside, labels[None, :], 0), axis=1)) - 1

def attend(inputs):
    shaped, starts, lengths = inputs
    queries = shaped[:, 0]
    keys = shaped[:, 1]
    values = shaped[:, 2]
    positions = jnp.arange(LEN, dtype=jnp.int32)
    labels = piece_labels(positions, starts, lengths)
    allowed = (positions[None, :] <= positions[:, None]) | (labels[:, None] == labels[None, :]) & (labels[:, None] >= 0)
    scores = low_back(jnp.einsum('qhe,khe->hqk', queries, keys, precision=lax.Precision.HIGHEST)) * 0.125
    scores = jnp.where(allowed[None], scores, negative)
    probs = low(jax.nn.softmax(scores, axis=-1))
    return jnp.einsum('hqk,khe->qhe', probs, values, precision=lax.Precision.HIGHEST)

def forward(values, starts, lengths):
    tokens, qkv_weight, query_bias, value_bias, out_weight, out_bias, gain_one, shift_one, in_weight, in_bias, back_weight, back_bias, gain_two, shift_two, reduce_weight, reduce_bias, pool_query, pool_weight, pool_bias, class_weight, class_bias = values
    shift_qkv = jnp.concatenate([query_bias, jnp.zeros_like(query_bias), value_bias])
    qkv = low(low_back(matmul(tokens, qkv_weight) + shift_qkv))
    shaped = qkv.reshape(SEQS, LEN, 3, H, HD)
    mixed = lax.map(jax.checkpoint(attend), (shaped, starts, lengths))
    mixed = low(low_back(mixed.reshape(SEQS, LEN, D)))
    attended = low_back(matmul(mixed, out_weight) + out_bias)
    first = layer_norm(tokens + attended, gain_one, shift_one)
    inner = low_back(matmul(low(first), in_weight) + in_bias)
    active = low(jax.nn.gelu(inner, approximate=False))
    branch = low_back(matmul(active, back_weight) + back_bias)
    result = low(layer_norm(first + branch, gain_two, shift_two))
    reduced = low_back(matmul(result, reduce_weight) + reduce_bias)
    pool_heads = reduced.reshape(SEQS, LEN, PH, RED // PH)
    query_rows = pool_query.reshape(PH, RED // PH)
    pool_scores = jnp.einsum('slpe,pe->slp', pool_heads, query_rows, precision=lax.Precision.HIGHEST) * 0.125
    pool_probs = jax.nn.softmax(pool_scores, axis=1)
    pooled = jnp.einsum('slp,slpe->spe', pool_probs, pool_heads, precision=lax.Precision.HIGHEST).reshape(SEQS, RED)
    hidden = jnp.tanh(matmul(pooled, pool_weight) + pool_bias)
    logits = matmul(hidden, class_weight) + class_bias
    return (result, logits)

def reference(tokens, out_grad, logit_grad, piece_start, piece_len, qkv_weight, query_bias, value_bias, out_weight, out_bias, gain_one, shift_one, in_weight, in_bias, back_weight, back_bias, gain_two, shift_two, reduce_weight, reduce_bias, pool_query, pool_weight, pool_bias, class_weight, class_bias):
    params = (tokens, qkv_weight, query_bias, value_bias, out_weight, out_bias, gain_one, shift_one, in_weight, in_bias, back_weight, back_bias, gain_two, shift_two, reduce_weight, reduce_bias, pool_query, pool_weight, pool_bias, class_weight, class_bias)
    floats = tuple((member.astype(jnp.float32) for member in params))

    def closed(*values):
        return forward(values, piece_start, piece_len)
    (layer_out, logits), pullback = jax.vjp(closed, *floats)
    grads = pullback((out_grad.astype(jnp.float32), logit_grad.astype(jnp.float32)))
    return (layer_out.astype(jnp.bfloat16), logits, grads[0].astype(jnp.bfloat16), grads[1], grads[2], grads[3], grads[4], grads[5], grads[6], grads[7], grads[8], grads[9], grads[10], grads[11], grads[12], grads[13], grads[14], grads[15], grads[16], grads[17], grads[18], grads[19], grads[20])
```

```python
from functools import partial

import jax
import jax.numpy as jnp
from jax import lax
from jax.sharding import PartitionSpec as P

H = 12
HD = 64
RED = 128
PH = 2
CLS = 14


negative = -1e30
epsilon = 1e-06
highest = lax.Precision.HIGHEST


def exchange(value, axis):
    size = lax.axis_size(axis)
    me = lax.axis_index(axis)
    result = value
    for step in range(1, size):
        other = (me + step) % size
        source = (me - step) % size
        sent = lax.dynamic_index_in_dim(value, other, 0, keepdims=False)
        came = lax.ppermute(sent, axis, [(k, (k + step) % size) for k in range(size)])
        result = lax.dynamic_update_index_in_dim(result, came, source, 0)
    return result


def summed_everywhere(value):
    for axis in ("dp", "ctx"):
        size = lax.axis_size(axis)
        step = 1
        while step < size:
            value = value + lax.ppermute(value, axis, [(k, k ^ step) for k in range(size)])
            step *= 2
    return value


def everyone(value):
    return lax.all_gather(value, ("dp", "ctx"), axis=0, tiled=True)


def to_owners(value):
    return lax.psum_scatter(value, ("dp", "ctx"), scatter_dimension=0, tiled=True)


def norm_rows(hidden, gain, shift):
    average = jnp.mean(hidden, axis=-1, keepdims=True)
    centred = hidden - average
    inv_std = lax.rsqrt(jnp.mean(centred * centred, axis=-1, keepdims=True) + epsilon)
    normed = centred * inv_std
    return (normed * gain + shift, normed, inv_std)


def norm_back(upstream, normed, inv_std, gain):
    scaled = upstream * gain
    first_mean = jnp.mean(scaled, axis=-1, keepdims=True)
    second = jnp.mean(scaled * normed, axis=-1, keepdims=True)
    return inv_std * (scaled - first_mean - normed * second)


def rows_product(left, right, precision=None):
    return lax.dot_general(
        left,
        right,
        (((0,), (0,)), ((), ())),
        precision=precision,
        preferred_element_type=jnp.float32,
    )


def right_transposed(left, right, precision=None):
    return lax.dot_general(
        left,
        right,
        (((1,), (1,)), ((), ())),
        precision=precision,
        preferred_element_type=jnp.float32,
    )


def piece_labels(positions, starts, lengths):
    inside = (positions[None, :, None] >= starts[:, None, :]) & (
        positions[None, :, None] < (starts + lengths)[:, None, :]
    )
    labels = jnp.arange(1, starts.shape[1] + 1, dtype=jnp.int32)
    return jnp.sum(jnp.where(inside, labels, 0), axis=2) - 1


def allowed_pairs(query_pos, key_pos, starts, lengths):
    query_label = piece_labels(query_pos, starts, lengths)
    key_label = piece_labels(key_pos, starts, lengths)
    causal = key_pos[None, None, :] <= query_pos[None, :, None]
    together = (query_label[:, :, None] == key_label[:, None, :]) & (query_label[:, :, None] >= 0)
    return (causal | together)[:, None]


def scores_of(queries, keys, allowed):
    raw_scores = (
        jnp.einsum("gqhe,gkhe->ghqk", queries, keys, preferred_element_type=jnp.float32) * 0.125
    )
    return jnp.where(allowed, raw_scores, negative)


def attend_block(query_pos, key_pos, inputs):
    queries, keys, values, starts, lengths = inputs
    scores = scores_of(queries, keys, allowed_pairs(query_pos, key_pos, starts, lengths))
    row_top = jnp.max(scores, axis=-1, keepdims=True)
    row_total = jnp.sum(jnp.exp(scores - row_top), axis=-1, keepdims=True)
    log_total = row_top + jnp.log(row_total)
    prob_low = jnp.exp(scores - log_total).astype(jnp.bfloat16)
    mixed_block = jnp.einsum(
        "ghqk,gkhe->gqhe", prob_low, values, preferred_element_type=jnp.float32
    )
    return (mixed_block.astype(jnp.bfloat16), log_total[..., 0])


def score_grads(
    query_pos, key_pos, queries, keys, values, starts, lengths, log_total, grad_mixed, centre
):
    scores = scores_of(queries, keys, allowed_pairs(query_pos, key_pos, starts, lengths))
    prob_full = jnp.exp(scores - log_total[..., None])
    grad_probs = jnp.einsum(
        "gqhe,gkhe->ghqk", grad_mixed, values, preferred_element_type=jnp.float32
    )
    centre = jnp.sum(prob_full * grad_probs, axis=-1)
    grad_scores = (prob_full * (grad_probs - centre[..., None]) * 0.125).astype(jnp.bfloat16)
    return (prob_full, grad_scores, centre)


def attend_back(query_pos, key_pos, inputs):
    queries, keys, values, starts, lengths, log_total, grad_mixed = inputs
    prob_full, grad_scores, centre = score_grads(
        query_pos, key_pos, queries, keys, values, starts, lengths, log_total, grad_mixed, None
    )
    grad_queries = jnp.einsum(
        "ghqk,gkhe->gqhe", grad_scores, keys, preferred_element_type=jnp.float32
    )
    grad_keys = jnp.einsum(
        "ghqk,gqhe->gkhe", grad_scores, queries, preferred_element_type=jnp.float32
    )
    grad_values = jnp.einsum(
        "ghqk,gqhe->gkhe",
        prob_full.astype(jnp.bfloat16),
        grad_mixed,
        preferred_element_type=jnp.float32,
    )
    return (grad_queries, grad_keys, grad_values)


def attention(positions, qkv_low, starts, lengths):
    length, width = qkv_low.shape[0], qkv_low.shape[1] // 3
    queries, keys, values = [
        qkv_low[:, k * width : (k + 1) * width].reshape(1, length, H, HD) for k in range(3)
    ]
    mixed, log_total = attend_block(positions, positions, (queries, keys, values, starts, lengths))
    return mixed.reshape(length, width), log_total


def attention_back(positions, qkv_low, starts, lengths, log_total, mixed_low, grad_mixed_low):
    length, width = mixed_low.shape
    queries, keys, values = [
        qkv_low[:, k * width : (k + 1) * width].reshape(1, length, H, HD) for k in range(3)
    ]
    grads = attend_back(
        positions,
        positions,
        (
            queries,
            keys,
            values,
            starts,
            lengths,
            log_total,
            grad_mixed_low.reshape(1, length, H, HD),
        ),
    )
    return jnp.concatenate(
        [grad.reshape(length, width).astype(jnp.bfloat16) for grad in grads], axis=1
    )


def interleave(rows, devices):
    width = rows.shape[1]
    part = rows.shape[0] // (4 * devices)
    split = rows.reshape(devices, 4, part, width)
    return jnp.swapaxes(split, 1, 2).reshape(devices * part, 4 * width)


def separate(columns, devices):
    width = columns.shape[1] // 4
    part = columns.shape[0] // devices
    split = columns.reshape(devices, part, 4, width)
    return jnp.swapaxes(split, 1, 2).reshape(devices * 4 * part, width)


def vector_columns(vectors, hidden_vector, devices):
    columns = [vector[:, None] for vector in vectors]
    columns.append(interleave(hidden_vector[:, None], devices))
    packed = jnp.concatenate(columns, axis=1)
    return jnp.pad(packed, ((0, 0), (0, 128 - packed.shape[1])))


def shards(
    tokens,
    out_grad,
    logit_grad,
    piece_start,
    piece_len,
    qkv_weight,
    query_bias,
    value_bias,
    out_weight,
    out_bias,
    gain_one,
    shift_one,
    in_weight,
    in_bias,
    back_weight,
    back_bias,
    gain_two,
    shift_two,
    reduce_weight,
    reduce_bias,
    pool_query,
    pool_weight,
    pool_bias,
    class_weight,
    class_bias,
):
    seq_count, local_len, width = tokens.shape
    ctx_size = lax.axis_size("ctx")
    assert seq_count == ctx_size
    devices = lax.axis_size("dp") * ctx_size
    hidden_units = in_weight.shape[1]
    assert hidden_units == 4 * width
    full_len = local_len * ctx_size
    head_width = RED // PH
    mine = lax.axis_index("ctx")
    positions = jnp.arange(full_len, dtype=jnp.int32)
    query_rows = pool_query.astype(jnp.float32).reshape(PH, head_width)
    pool_weight_f = pool_weight.astype(jnp.float32)
    class_weight_f = class_weight.astype(jnp.float32)
    reduce_shift = reduce_bias.astype(jnp.float32)
    pool_shift = pool_bias.astype(jnp.float32)
    class_shift = class_bias.astype(jnp.float32)
    starts = lax.dynamic_slice_in_dim(piece_start, mine, 1, 0)
    lengths = lax.dynamic_slice_in_dim(piece_len, mine, 1, 0)
    logit_row = lax.dynamic_slice_in_dim(logit_grad, mine, 1, 0)

    small = vector_columns(
        (query_bias, value_bias, out_bias, gain_one, shift_one, back_bias, gain_two, shift_two),
        in_bias,
        1,
    )
    early = everyone(jnp.concatenate([qkv_weight, small], axis=1))
    late = everyone(
        jnp.concatenate(
            [out_weight, in_weight, interleave(back_weight, 1), reduce_weight], axis=1
        )
    )
    seq_tokens = exchange(tokens, "ctx").reshape(full_len, width)
    seq_out_grad = exchange(out_grad, "ctx").reshape(full_len, width)

    qkv_full = early[:, : 3 * width]
    vectors = early[:, 3 * width :].astype(jnp.float32)
    q_bias, v_bias, o_bias, g_one, s_one, b_bias, g_two, s_two = [vectors[:, k] for k in range(8)]
    i_bias = separate(vectors[:, 8:12], devices)[:, 0]
    out_full = late[:, :width]
    in_full = late[:, width : 5 * width]
    back_full = separate(late[:, 5 * width : 9 * width], devices)
    reduce_full = late[:, 9 * width :]

    qkv_shift = jnp.concatenate([q_bias, jnp.zeros_like(q_bias), v_bias])
    qkv_low = (
        jnp.dot(seq_tokens, qkv_full, preferred_element_type=jnp.float32) + qkv_shift
    ).astype(jnp.bfloat16)
    mixed_low, log_total = attention(positions, qkv_low, starts, lengths)
    attended = jnp.dot(mixed_low, out_full, preferred_element_type=jnp.float32) + o_bias
    first_norm, normed_one, inv_one = norm_rows(
        seq_tokens.astype(jnp.float32) + attended, g_one, s_one
    )
    first_low = first_norm.astype(jnp.bfloat16)
    inner_pre = jnp.dot(first_low, in_full, preferred_element_type=jnp.float32) + i_bias
    active, gelu_back = jax.vjp(partial(jax.nn.gelu, approximate=False), inner_pre)
    active_low = active.astype(jnp.bfloat16)
    branch = jnp.dot(active_low, back_full, preferred_element_type=jnp.float32) + b_bias
    result, normed_two, inv_two = norm_rows(first_norm + branch, g_two, s_two)
    result_low = result.astype(jnp.bfloat16)
    layer_out = exchange(result_low.reshape(ctx_size, local_len, width), "ctx")
    reduced = jnp.dot(result_low, reduce_full, preferred_element_type=jnp.float32) + reduce_shift
    pool_heads = reduced.reshape(full_len, PH, head_width)
    pool_scores = jnp.einsum("lpe,pe->lp", pool_heads, query_rows, precision=highest) * 0.125
    pool_top = jnp.max(pool_scores, axis=0)
    pool_exp = jnp.exp(pool_scores - pool_top)
    pool_total = jnp.sum(pool_exp, axis=0)
    pool_probs = pool_exp / pool_total
    pooled_heads = jnp.einsum("lp,lpe->pe", pool_probs, pool_heads, precision=highest)
    pooled = pooled_heads.reshape(1, RED)
    hidden = jnp.tanh(jnp.dot(pooled, pool_weight_f, precision=highest) + pool_shift)
    logit_mine = jnp.dot(hidden, class_weight_f, precision=highest) + class_shift
    logits = exchange(jnp.broadcast_to(logit_mine[None], (ctx_size, 1, CLS)), "ctx")[:, 0]

    grad_class = rows_product(hidden, logit_row, highest)
    grad_class_bias = jnp.sum(logit_row, axis=0)
    grad_hidden = right_transposed(logit_row, class_weight_f, highest)
    grad_pre = grad_hidden * (1.0 - hidden * hidden)
    grad_pool_weight = rows_product(pooled, grad_pre, highest)
    grad_pool_bias = jnp.sum(grad_pre, axis=0)
    grad_pooled = right_transposed(grad_pre, pool_weight_f, highest).reshape(PH, head_width)
    pool_along = jnp.einsum(
        "lpe,pe->lp", pool_heads, grad_pooled, precision=highest
    ) - jnp.sum(pooled_heads * grad_pooled, axis=-1)
    grad_pool_scores = pool_probs * pool_along
    grad_reduced = (
        pool_probs[..., None] * grad_pooled + grad_pool_scores[..., None] * query_rows * 0.125
    )
    grad_query = (
        jnp.einsum("lp,lpe->pe", grad_pool_scores, pool_heads, precision=highest).reshape(RED)
        * 0.125
    )
    grad_red_low = grad_reduced.reshape(full_len, RED).astype(jnp.bfloat16)
    grad_reduce_bias = jnp.sum(grad_red_low.astype(jnp.float32), axis=0)
    tiny = summed_everywhere(
        jnp.concatenate(
            [
                grad_pool_weight,
                jnp.pad(grad_class.T, ((0, 16 - CLS), (0, 0))),
                jnp.pad(grad_class_bias, (0, RED - CLS))[None],
                grad_pool_bias[None],
                grad_query[None],
                grad_reduce_bias[None],
                jnp.zeros((4, RED), jnp.float32),
            ],
            axis=0,
        )
    )
    grad_reduce = rows_product(result_low, grad_red_low)
    grad_result = seq_out_grad.astype(jnp.float32) + right_transposed(grad_red_low, reduce_full)
    grad_gain_two = jnp.sum(grad_result * normed_two, axis=0)
    grad_shift_two = jnp.sum(grad_result, axis=0)
    grad_mid = norm_back(grad_result, normed_two, inv_two, g_two)
    grad_branch_low = grad_mid.astype(jnp.bfloat16)
    grad_back_bias = jnp.sum(grad_branch_low.astype(jnp.float32), axis=0)
    grad_back = rows_product(active_low, grad_branch_low)
    grad_active = right_transposed(grad_branch_low, back_full)
    grad_inner_low = gelu_back(grad_active)[0].astype(jnp.bfloat16)
    grad_in_bias = jnp.sum(grad_inner_low.astype(jnp.float32), axis=0)
    grad_in = rows_product(first_low, grad_inner_low)
    early_owned = to_owners(
        jnp.concatenate(
            [
                grad_in.astype(jnp.bfloat16),
                interleave(grad_back.astype(jnp.bfloat16), devices),
                grad_reduce.astype(jnp.bfloat16),
            ],
            axis=1,
        )
    ).astype(jnp.float32)
    grad_first = grad_mid + right_transposed(grad_inner_low, in_full)
    grad_gain_one = jnp.sum(grad_first * normed_one, axis=0)
    grad_shift_one = jnp.sum(grad_first, axis=0)
    grad_start = norm_back(grad_first, normed_one, inv_one, g_one)
    grad_attn_low = grad_start.astype(jnp.bfloat16)
    grad_out_bias = jnp.sum(grad_attn_low.astype(jnp.float32), axis=0)
    grad_out = rows_product(mixed_low, grad_attn_low)
    grad_mixed_low = right_transposed(grad_attn_low, out_full).astype(jnp.bfloat16)
    grad_qkv_low = attention_back(
        positions, qkv_low, starts, lengths, log_total, mixed_low, grad_mixed_low
    )
    grad_query_bias = jnp.sum(grad_qkv_low[:, :width].astype(jnp.float32), axis=0)
    grad_value_bias = jnp.sum(grad_qkv_low[:, 2 * width :].astype(jnp.float32), axis=0)
    grad_qkv = rows_product(seq_tokens, grad_qkv_low)
    grad_small = vector_columns(
        (
            grad_query_bias,
            grad_value_bias,
            grad_out_bias,
            grad_gain_one,
            grad_shift_one,
            grad_back_bias,
            grad_gain_two,
            grad_shift_two,
        ),
        grad_in_bias,
        devices,
    )
    late_owned = to_owners(
        jnp.concatenate(
            [
                grad_qkv.astype(jnp.bfloat16),
                grad_out.astype(jnp.bfloat16),
                grad_small.astype(jnp.bfloat16),
            ],
            axis=1,
        )
    ).astype(jnp.float32)
    token_grad = (grad_start + right_transposed(grad_qkv_low, qkv_full)).astype(jnp.bfloat16)
    token_grad = exchange(token_grad.reshape(ctx_size, local_len, width), "ctx")
    small_owned = late_owned[:, 4 * width :]
    tall = RED + 16
    return (
        layer_out,
        logits,
        token_grad,
        late_owned[:, : 3 * width],
        small_owned[:, 0],
        small_owned[:, 1],
        late_owned[:, 3 * width : 4 * width],
        small_owned[:, 2],
        small_owned[:, 3],
        small_owned[:, 4],
        early_owned[:, : 4 * width],
        separate(small_owned[:, 8:12], 1)[:, 0],
        separate(early_owned[:, 4 * width : 8 * width], 1),
        small_owned[:, 5],
        small_owned[:, 6],
        small_owned[:, 7],
        early_owned[:, 8 * width :],
        tiny[tall + 3],
        tiny[tall + 2],
        tiny[:RED],
        tiny[tall + 1],
        tiny[RED : RED + CLS].T,
        tiny[tall, :CLS],
    )


def solution(mesh):
    placed = (
        P("dp", "ctx", None),
        P("dp", "ctx", None),
        P("dp", None),
        P("dp", None),
        P("dp", None),
        P(("dp", "ctx"), None),
        P(("dp", "ctx")),
        P(("dp", "ctx")),
        P(("dp", "ctx"), None),
        P(("dp", "ctx")),
        P(("dp", "ctx")),
        P(("dp", "ctx")),
        P(("dp", "ctx"), None),
        P(("dp", "ctx")),
        P(("dp", "ctx"), None),
        P(("dp", "ctx")),
        P(("dp", "ctx")),
        P(("dp", "ctx")),
        P(("dp", "ctx"), None),
        P(),
        P(),
        P(),
        P(),
        P(),
        P(),
    )
    return jax.shard_map(
        shards,
        mesh=mesh,
        in_specs=placed,
        out_specs=(
            P("dp", "ctx", None),
            P("dp", None),
            P("dp", "ctx", None),
            P(("dp", "ctx"), None),
            P(("dp", "ctx")),
            P(("dp", "ctx")),
            P(("dp", "ctx"), None),
            P(("dp", "ctx")),
            P(("dp", "ctx")),
            P(("dp", "ctx")),
            P(("dp", "ctx"), None),
            P(("dp", "ctx")),
            P(("dp", "ctx"), None),
            P(("dp", "ctx")),
            P(("dp", "ctx")),
            P(("dp", "ctx")),
            P(("dp", "ctx"), None),
            P(),
            P(),
            P(),
            P(),
            P(),
            P(),
        ),
        check_vma=False,
    )
```

```python
from functools import partial

import jax
import jax.numpy as jnp
from jax import lax
from jax.experimental import pallas as pl
from jax.experimental.pallas import tpu as pltpu
from jax.sharding import PartitionSpec as P

H = 12
HD = 64
RED = 128
PH = 2
CLS = 14


negative = -1e30
epsilon = 1e-06
highest = lax.Precision.HIGHEST


def exchange(value, axis):
    size = lax.axis_size(axis)
    me = lax.axis_index(axis)
    result = value
    for step in range(1, size):
        other = (me + step) % size
        source = (me - step) % size
        sent = lax.dynamic_index_in_dim(value, other, 0, keepdims=False)
        came = lax.ppermute(sent, axis, [(k, (k + step) % size) for k in range(size)])
        result = lax.dynamic_update_index_in_dim(result, came, source, 0)
    return result


def summed_everywhere(value):
    for axis in ("dp", "ctx"):
        size = lax.axis_size(axis)
        step = 1
        while step < size:
            value = value + lax.ppermute(value, axis, [(k, k ^ step) for k in range(size)])
            step *= 2
    return value


def device_bits():
    bits = []
    for axis in ("dp", "ctx"):
        size = lax.axis_size(axis)
        stride = size // 2
        while stride:
            bits.append((axis, stride, size))
            stride //= 2
    return bits


def bit_orders(bits, count):
    partner = ("dp", 1, lax.axis_size("dp"))
    others = [k for k, bit in enumerate(bits) if bit != partner]
    orders = []
    for turn in range(count):
        cut = (len(others) - turn) % len(others)
        orders.append(others[cut:] + others[:cut] + [bits.index(partner)])
    return orders


def my_bit(bit):
    axis, stride, _ = bit
    return (lax.axis_index(axis) // stride) % 2


def swap(value, bit):
    axis, stride, size = bit
    return lax.ppermute(value, axis, [(k, k ^ stride) for k in range(size)])


def everyone(chunks):
    bits = device_bits()
    orders = bit_orders(bits, len(chunks))
    parts = list(chunks)
    for turn in range(len(bits)):
        for k, order in enumerate(orders):
            bit = bits[order[turn]]
            mine, other = parts[k], swap(parts[k], bit)
            low = my_bit(bit) == 0
            parts[k] = jnp.where(low, jnp.stack([mine, other]), jnp.stack([other, mine]))
    whole = []
    for part, order, chunk in zip(parts, orders, chunks):
        placed = order[::-1]
        axes = [placed.index(k) for k in range(len(bits))]
        whole.append(
            jnp.transpose(part, axes + [len(bits), len(bits) + 1]).reshape(-1, chunk.shape[1])
        )
    return whole


def to_owners(chunks):
    bits = device_bits()
    orders = [order[::-1] for order in bit_orders(bits, len(chunks))]
    devices = 2 ** len(bits)
    parts = [
        chunk.reshape([2] * len(bits) + [chunk.shape[0] // devices, chunk.shape[1]])
        for chunk in chunks
    ]
    left = [list(range(len(bits))) for _ in chunks]
    for turn in range(len(bits)):
        for k, order in enumerate(orders):
            axis = left[k].index(order[turn])
            bit = bits[order[turn]]
            side = my_bit(bit)
            sent = lax.dynamic_index_in_dim(parts[k], 1 - side, axis, keepdims=False)
            kept = lax.dynamic_index_in_dim(parts[k], side, axis, keepdims=False)
            came = swap(sent, bit)
            total = kept.astype(jnp.float32) + came.astype(jnp.float32)
            parts[k] = total if turn == len(bits) - 1 else total.astype(jnp.bfloat16)
            left[k].remove(order[turn])
    return parts


def norm_rows(hidden, gain, shift):
    average = jnp.mean(hidden, axis=-1, keepdims=True)
    centred = hidden - average
    inv_std = lax.rsqrt(jnp.mean(centred * centred, axis=-1, keepdims=True) + epsilon)
    normed = centred * inv_std
    return (normed * gain + shift, normed, inv_std)


def norm_back(upstream, normed, inv_std, gain):
    scaled = upstream * gain
    first_mean = jnp.mean(scaled, axis=-1, keepdims=True)
    second = jnp.mean(scaled * normed, axis=-1, keepdims=True)
    return inv_std * (scaled - first_mean - normed * second)


def rows_product(left, right, precision=None):
    return lax.dot_general(
        left,
        right,
        (((0,), (0,)), ((), ())),
        precision=precision,
        preferred_element_type=jnp.float32,
    )


def right_transposed(left, right, precision=None):
    return lax.dot_general(
        left,
        right,
        (((1,), (1,)), ((), ())),
        precision=precision,
        preferred_element_type=jnp.float32,
    )


def fill_bias(starts_ref, lengths_ref, bias_ref):
    regions, region, _ = bias_ref.shape
    for r in range(regions):
        key = lax.broadcasted_iota(jnp.int32, (region, region), 0)
        query = lax.broadcasted_iota(jnp.int32, (region, region), 1)
        low = starts_ref[0, r] - r * region
        high = low + lengths_ref[0, r]
        together = (key >= low) & (key < high) & (query >= low) & (query < high)
        bias_ref[r] = jnp.where((key <= query) | together, 0.0, negative)


def head_lanes(block, head):
    lane = lax.broadcasted_iota(jnp.int32, block.shape, 1)
    return jnp.where(lane // HD == head, block, jnp.zeros_like(block))


def plain_dot(left, right):
    return jnp.dot(left, right, preferred_element_type=jnp.float32)


def attention_kernel(
    starts_ref, lengths_ref, query_ref, key_ref, value_ref, mixed_ref, total_ref, bias_ref, *, span
):
    @pl.when(pl.program_id(0) == 0)
    def _():
        fill_bias(starts_ref, lengths_ref, bias_ref)

    length, lanes = query_ref.shape
    region = bias_ref.shape[1]
    queries_t = (query_ref[...] * 0.125).T
    values_t = value_ref[...].T
    heads = []
    for head in range(lanes // HD):
        keys = head_lanes(key_ref[...], head)
        rows = slice(head * HD, (head + 1) * HD)
        blocks = []
        for begin in range(0, length, span):
            r = begin // region
            reach = (r + 1) * region
            scores = plain_dot(keys[:reach], queries_t[:, begin : begin + span])
            inner = begin - r * region
            last = scores[reach - region :] + bias_ref[r, :, inner : inner + span]
            scores = jnp.concatenate([scores[: reach - region], last]) if r else last
            top = jnp.max(scores, axis=0, keepdims=True)
            weights = jnp.exp(scores - top)
            total = jnp.sum(weights, axis=0, keepdims=True)
            mixed_t = plain_dot(values_t[rows, :reach], weights.astype(jnp.bfloat16))
            blocks.append(mixed_t * (1.0 / total))
            total_ref[0, head : head + 1, begin : begin + span] = top + jnp.log(total)
        heads.append(jnp.concatenate(blocks, axis=1))
    mixed_ref[...] = jnp.concatenate(heads, axis=0).astype(jnp.bfloat16).T


def attention_back_kernel(
    starts_ref,
    lengths_ref,
    query_ref,
    key_ref,
    value_ref,
    total_ref,
    mixed_ref,
    upstream_ref,
    query_grad_ref,
    key_grad_ref,
    value_grad_ref,
    query_sum_ref,
    value_sum_ref,
    bias_ref,
    *,
    span,
):
    @pl.when(pl.program_id(0) == 0)
    def _():
        fill_bias(starts_ref, lengths_ref, bias_ref)

    length, lanes = query_ref.shape
    region = bias_ref.shape[1]
    queries = query_ref[...] * 0.125
    queries_t = queries.T
    keys_t = key_ref[...].T
    upstream = upstream_ref[...]
    upstream_t = upstream.T
    products = (upstream_t.astype(jnp.float32) * mixed_ref[...].T.astype(jnp.float32))
    query_heads = []
    key_grad = None
    value_grad = None
    lane = lax.broadcasted_iota(jnp.int32, (length, lanes), 1)
    for head in range(lanes // HD):
        keys = head_lanes(key_ref[...], head)
        values = head_lanes(value_ref[...], head)
        rows = slice(head * HD, (head + 1) * HD)
        centre = jnp.sum(products[rows], axis=0, keepdims=True)
        key_parts = [None] * (length // region)
        value_parts = [None] * (length // region)
        blocks = []
        for begin in range(0, length, span):
            r = begin // region
            reach = (r + 1) * region
            here = slice(begin, begin + span)
            scores = plain_dot(keys[:reach], queries_t[:, here])
            inner = begin - r * region
            last = scores[reach - region :] + bias_ref[r, :, inner : inner + span]
            scores = jnp.concatenate([scores[: reach - region], last]) if r else last
            probs = jnp.exp(scores - total_ref[0, head : head + 1, here])
            grad_probs = plain_dot(values[:reach], upstream_t[:, here])
            grad_scores = (probs * (grad_probs - centre[:, here])).astype(jnp.bfloat16)
            probs_low = probs.astype(jnp.bfloat16)
            value_term = plain_dot(probs_low, upstream[here])
            key_term = plain_dot(grad_scores, queries[here])
            for k in range(r + 1):
                part = slice(k * region, (k + 1) * region)
                first = key_parts[k] is None
                key_parts[k] = key_term[part] if first else key_parts[k] + key_term[part]
                value_parts[k] = value_term[part] if first else value_parts[k] + value_term[part]
            blocks.append(plain_dot(keys_t[rows, :reach], grad_scores))
        query_heads.append(jnp.concatenate(blocks, axis=1))
        key_head = jnp.concatenate(key_parts, axis=0)
        value_head = jnp.concatenate(value_parts, axis=0)
        mine = lane // HD == head
        key_grad = key_head if head == 0 else jnp.where(mine, key_head, key_grad)
        value_grad = value_head if head == 0 else jnp.where(mine, value_head, value_grad)
    query_low = (jnp.concatenate(query_heads, axis=0) * 0.125).astype(jnp.bfloat16).T
    value_low = value_grad.astype(jnp.bfloat16)
    query_grad_ref[...] = query_low
    key_grad_ref[...] = key_grad.astype(jnp.bfloat16)
    value_grad_ref[...] = value_low
    query_sum_ref[0] = jnp.sum(query_low.astype(jnp.float32), axis=0, keepdims=True)
    value_sum_ref[0] = jnp.sum(value_low.astype(jnp.float32), axis=0, keepdims=True)


def attention_specs(length, regions):
    column = pl.BlockSpec((length, 2 * HD), lambda i: (0, i))
    totals = pl.BlockSpec((1, 2, length), lambda i: (i, 0, 0))
    sums = pl.BlockSpec((1, 1, 2 * HD), lambda i: (i, 0, 0))
    scalars = pl.BlockSpec(memory_space=pltpu.SMEM)
    bias = pltpu.VMEM((regions, length // regions, length // regions), jnp.float32)
    return column, totals, sums, scalars, bias


def attention(queries, keys, values, starts, lengths):
    length, width = queries.shape
    regions = starts.shape[1]
    column, totals, sums, scalars, bias = attention_specs(length, regions)
    return pl.pallas_call(
        partial(attention_kernel, span=length // regions),
        grid=(H // 2,),
        in_specs=[scalars, scalars, column, column, column],
        out_specs=[column, totals],
        out_shape=[
            jax.ShapeDtypeStruct((length, width), jnp.bfloat16),
            jax.ShapeDtypeStruct((H // 2, 2, length), jnp.float32),
        ],
        scratch_shapes=[bias],
        name="attention",
    )(starts, lengths, queries, keys, values)


def attention_back(queries, keys, values, starts, lengths, log_total, mixed, upstream):
    length, width = queries.shape
    regions = starts.shape[1]
    column, totals, sums, scalars, bias = attention_specs(length, regions)
    grad = jax.ShapeDtypeStruct((length, width), jnp.bfloat16)
    grad_sum = jax.ShapeDtypeStruct((H // 2, 1, 2 * HD), jnp.float32)
    return pl.pallas_call(
        partial(attention_back_kernel, span=length // regions),
        grid=(H // 2,),
        in_specs=[scalars, scalars, column, column, column, totals, column, column],
        out_specs=[column, column, column, sums, sums],
        out_shape=[grad, grad, grad, grad_sum, grad_sum],
        scratch_shapes=[bias],
        name="attention_back",
    )(starts, lengths, queries, keys, values, log_total, mixed, upstream)


def interleave(rows, devices):
    width = rows.shape[1]
    part = rows.shape[0] // (4 * devices)
    split = rows.reshape(devices, 4, part, width)
    return jnp.swapaxes(split, 1, 2).reshape(devices * part, 4 * width)


def separate(columns, devices):
    width = columns.shape[1] // 4
    part = columns.shape[0] // devices
    split = columns.reshape(devices, part, 4, width)
    return jnp.swapaxes(split, 1, 2).reshape(devices * 4 * part, width)


def vector_columns(vectors, hidden_vector, devices):
    columns = [vector[:, None] for vector in vectors]
    columns.append(interleave(hidden_vector[:, None], devices))
    packed = jnp.concatenate(columns, axis=1)
    return jnp.pad(packed, ((0, 0), (0, 128 - packed.shape[1])))


def shards(
    tokens,
    out_grad,
    logit_grad,
    piece_start,
    piece_len,
    qkv_weight,
    query_bias,
    value_bias,
    out_weight,
    out_bias,
    gain_one,
    shift_one,
    in_weight,
    in_bias,
    back_weight,
    back_bias,
    gain_two,
    shift_two,
    reduce_weight,
    reduce_bias,
    pool_query,
    pool_weight,
    pool_bias,
    class_weight,
    class_bias,
):
    seq_count, local_len, width = tokens.shape
    ctx_size = lax.axis_size("ctx")
    assert seq_count == ctx_size
    devices = lax.axis_size("dp") * ctx_size
    hidden_units = in_weight.shape[1]
    assert hidden_units == 4 * width
    full_len = local_len * ctx_size
    head_width = RED // PH
    mine = lax.axis_index("ctx")
    query_rows = pool_query.astype(jnp.float32).reshape(PH, head_width)
    pool_weight_f = pool_weight.astype(jnp.float32)
    class_weight_f = class_weight.astype(jnp.float32)
    reduce_shift = reduce_bias.astype(jnp.float32)
    pool_shift = pool_bias.astype(jnp.float32)
    class_shift = class_bias.astype(jnp.float32)
    starts = lax.dynamic_slice_in_dim(piece_start, mine, 1, 0)
    lengths = lax.dynamic_slice_in_dim(piece_len, mine, 1, 0)
    logit_row = lax.dynamic_slice_in_dim(logit_grad, mine, 1, 0)

    small = vector_columns(
        (query_bias, value_bias, out_bias, gain_one, shift_one, back_bias, gain_two, shift_two),
        in_bias,
        1,
    )
    half = width // 2
    early = everyone(
        [
            jnp.concatenate([qkv_weight[:, :width], small, reduce_weight], axis=1),
            jnp.concatenate([qkv_weight[:, width : 2 * width], out_weight[:, :half]], axis=1),
            jnp.concatenate([qkv_weight[:, 2 * width :], out_weight[:, half:]], axis=1),
        ]
    )
    part = in_weight.shape[0]
    late = lax.all_gather(
        jnp.concatenate(
            [in_weight[:, k * width : (k + 1) * width] for k in range(4)] + [back_weight], axis=0
        ),
        ("dp", "ctx"),
        axis=0,
    )
    seq_tokens = exchange(tokens, "ctx").reshape(full_len, width)
    query_weight = early[0][:, :width]
    key_weight = early[1][:, :width]
    value_weight = early[2][:, :width]
    out_full = jnp.concatenate([early[1][:, width:], early[2][:, width:]], axis=1)
    reduce_full = early[0][:, width + 128 :]
    vectors = early[0][:, width : width + 128].astype(jnp.float32)
    q_bias, v_bias, o_bias, g_one, s_one, b_bias, g_two, s_two = [vectors[:, k] for k in range(8)]
    i_bias = separate(vectors[:, 8:12], devices)[:, 0]
    in_full = jnp.concatenate(
        [late[:, k * part : (k + 1) * part].reshape(width, width) for k in range(4)], axis=1
    )
    back_full = late[:, 4 * part :].reshape(hidden_units, width)

    def project(weight):
        return jnp.dot(seq_tokens, weight, preferred_element_type=jnp.float32)

    queries = (project(query_weight) + q_bias).astype(jnp.bfloat16)
    keys = project(key_weight).astype(jnp.bfloat16)
    values = (project(value_weight) + v_bias).astype(jnp.bfloat16)
    out_grad, queries = lax.optimization_barrier((out_grad, queries))
    seq_out_grad = exchange(out_grad, "ctx").reshape(full_len, width)
    mixed_low, log_total = attention(queries, keys, values, starts, lengths)
    attended = jnp.dot(mixed_low, out_full, preferred_element_type=jnp.float32) + o_bias
    first_norm, normed_one, inv_one = norm_rows(
        seq_tokens.astype(jnp.float32) + attended, g_one, s_one
    )
    first_low = first_norm.astype(jnp.bfloat16)
    inner_pre = jnp.dot(first_low, in_full, preferred_element_type=jnp.float32) + i_bias
    active, gelu_back = jax.vjp(partial(jax.nn.gelu, approximate=False), inner_pre)
    active_low = active.astype(jnp.bfloat16)
    branch = jnp.dot(active_low, back_full, preferred_element_type=jnp.float32) + b_bias
    result, normed_two, inv_two = norm_rows(first_norm + branch, g_two, s_two)
    result_low = result.astype(jnp.bfloat16)
    layer_out = exchange(result_low.reshape(ctx_size, local_len, width), "ctx")
    reduced = jnp.dot(result_low, reduce_full, preferred_element_type=jnp.float32) + reduce_shift
    pool_heads = reduced.reshape(full_len, PH, head_width)
    pool_scores = jnp.einsum("lpe,pe->lp", pool_heads, query_rows, precision=highest) * 0.125
    pool_top = jnp.max(pool_scores, axis=0)
    pool_exp = jnp.exp(pool_scores - pool_top)
    pool_total = jnp.sum(pool_exp, axis=0)
    pool_probs = pool_exp / pool_total
    pooled_heads = jnp.einsum("lp,lpe->pe", pool_probs, pool_heads, precision=highest)
    pooled = pooled_heads.reshape(1, RED)
    hidden = jnp.tanh(jnp.dot(pooled, pool_weight_f, precision=highest) + pool_shift)
    logit_mine = jnp.dot(hidden, class_weight_f, precision=highest) + class_shift
    logits = exchange(jnp.broadcast_to(logit_mine[None], (ctx_size, 1, CLS)), "ctx")[:, 0]

    grad_class = rows_product(hidden, logit_row, highest)
    grad_class_bias = jnp.sum(logit_row, axis=0)
    grad_hidden = right_transposed(logit_row, class_weight_f, highest)
    grad_pre = grad_hidden * (1.0 - hidden * hidden)
    grad_pool_weight = rows_product(pooled, grad_pre, highest)
    grad_pool_bias = jnp.sum(grad_pre, axis=0)
    grad_pooled = right_transposed(grad_pre, pool_weight_f, highest).reshape(PH, head_width)
    pool_along = jnp.einsum(
        "lpe,pe->lp", pool_heads, grad_pooled, precision=highest
    ) - jnp.sum(pooled_heads * grad_pooled, axis=-1)
    grad_pool_scores = pool_probs * pool_along
    grad_reduced = (
        pool_probs[..., None] * grad_pooled + grad_pool_scores[..., None] * query_rows * 0.125
    )
    grad_query = (
        jnp.einsum("lp,lpe->pe", grad_pool_scores, pool_heads, precision=highest).reshape(RED)
        * 0.125
    )
    grad_red_low = grad_reduced.reshape(full_len, RED).astype(jnp.bfloat16)
    grad_reduce_bias = jnp.sum(grad_red_low.astype(jnp.float32), axis=0)
    tiny = summed_everywhere(
        jnp.concatenate(
            [
                grad_pool_weight,
                jnp.pad(grad_class.T, ((0, 16 - CLS), (0, 0))),
                jnp.pad(grad_class_bias, (0, RED - CLS))[None],
                grad_pool_bias[None],
                grad_query[None],
                grad_reduce_bias[None],
                jnp.zeros((4, RED), jnp.float32),
            ],
            axis=0,
        )
    )
    grad_reduce = rows_product(result_low, grad_red_low)
    grad_result = seq_out_grad.astype(jnp.float32) + right_transposed(grad_red_low, reduce_full)
    grad_gain_two = jnp.sum(grad_result * normed_two, axis=0)
    grad_shift_two = jnp.sum(grad_result, axis=0)
    grad_mid = norm_back(grad_result, normed_two, inv_two, g_two)
    grad_branch_low = grad_mid.astype(jnp.bfloat16)
    grad_back_bias = jnp.sum(grad_branch_low.astype(jnp.float32), axis=0)
    grad_back = rows_product(active_low, grad_branch_low)
    grad_active = right_transposed(grad_branch_low, back_full)
    grad_inner_low = gelu_back(grad_active)[0].astype(jnp.bfloat16)
    grad_in_bias = jnp.sum(grad_inner_low.astype(jnp.float32), axis=0)
    grad_in = rows_product(first_low, grad_inner_low)
    grad_in = grad_in.astype(jnp.bfloat16)
    packed = jnp.concatenate(
        [grad_in[:, k * width : (k + 1) * width].reshape(devices, part, width) for k in range(4)]
        + [grad_back.astype(jnp.bfloat16).reshape(devices, 4 * part, width)],
        axis=1,
    )
    packed, grad_inner_low = lax.optimization_barrier((packed, grad_inner_low))
    early_owned = lax.psum_scatter(
        packed.reshape(devices * 8 * part, width), ("dp", "ctx"), scatter_dimension=0, tiled=True
    ).astype(jnp.float32)
    grad_first = grad_mid + right_transposed(grad_inner_low, in_full)
    grad_gain_one = jnp.sum(grad_first * normed_one, axis=0)
    grad_shift_one = jnp.sum(grad_first, axis=0)
    grad_start = norm_back(grad_first, normed_one, inv_one, g_one)
    grad_attn_low = grad_start.astype(jnp.bfloat16)
    grad_out_bias = jnp.sum(grad_attn_low.astype(jnp.float32), axis=0)
    grad_out = rows_product(mixed_low, grad_attn_low)
    grad_mixed_low = right_transposed(grad_attn_low, out_full).astype(jnp.bfloat16)
    query_grad, key_grad, value_grad, query_sum, value_sum = attention_back(
        queries, keys, values, starts, lengths, log_total, mixed_low, grad_mixed_low
    )
    grad_query_bias = query_sum.reshape(width)
    grad_value_bias = value_sum.reshape(width)
    grad_small = vector_columns(
        (
            grad_query_bias,
            grad_value_bias,
            grad_out_bias,
            grad_gain_one,
            grad_shift_one,
            grad_back_bias,
            grad_gain_two,
            grad_shift_two,
        ),
        grad_in_bias,
        devices,
    )
    grad_out = grad_out.astype(jnp.bfloat16)

    def weight_grad(upstream):
        return rows_product(seq_tokens, upstream).astype(jnp.bfloat16)

    late_owned = to_owners(
        [
            jnp.concatenate(
                [
                    weight_grad(query_grad),
                    grad_small.astype(jnp.bfloat16),
                    grad_reduce.astype(jnp.bfloat16),
                ],
                axis=1,
            ),
            jnp.concatenate([weight_grad(key_grad), grad_out[:, :half]], axis=1),
            jnp.concatenate([weight_grad(value_grad), grad_out[:, half:]], axis=1),
        ]
    )
    token_grad = (
        grad_start
        + right_transposed(query_grad, query_weight)
        + right_transposed(key_grad, key_weight)
        + right_transposed(value_grad, value_weight)
    ).astype(jnp.bfloat16)
    token_grad = exchange(token_grad.reshape(ctx_size, local_len, width), "ctx")
    small_owned = late_owned[0][:, width : width + 128]
    tall = RED + 16
    return (
        layer_out,
        logits,
        token_grad,
        jnp.concatenate([owned[:, :width] for owned in late_owned], axis=1),
        small_owned[:, 0],
        small_owned[:, 1],
        jnp.concatenate([late_owned[1][:, width:], late_owned[2][:, width:]], axis=1),
        small_owned[:, 2],
        small_owned[:, 3],
        small_owned[:, 4],
        jnp.concatenate([early_owned[k * part : (k + 1) * part] for k in range(4)], axis=1),
        separate(small_owned[:, 8:12], 1)[:, 0],
        early_owned[4 * part :],
        small_owned[:, 5],
        small_owned[:, 6],
        small_owned[:, 7],
        late_owned[0][:, width + 128 :],
        tiny[tall + 3],
        tiny[tall + 2],
        tiny[:RED],
        tiny[tall + 1],
        tiny[RED : RED + CLS].T,
        tiny[tall, :CLS],
    )


def solution(mesh):
    placed = (
        P("dp", "ctx", None),
        P("dp", "ctx", None),
        P("dp", None),
        P("dp", None),
        P("dp", None),
        P(("dp", "ctx"), None),
        P(("dp", "ctx")),
        P(("dp", "ctx")),
        P(("dp", "ctx"), None),
        P(("dp", "ctx")),
        P(("dp", "ctx")),
        P(("dp", "ctx")),
        P(("dp", "ctx"), None),
        P(("dp", "ctx")),
        P(("dp", "ctx"), None),
        P(("dp", "ctx")),
        P(("dp", "ctx")),
        P(("dp", "ctx")),
        P(("dp", "ctx"), None),
        P(),
        P(),
        P(),
        P(),
        P(),
        P(),
    )
    return jax.shard_map(
        shards,
        mesh=mesh,
        in_specs=placed,
        out_specs=(
            P("dp", "ctx", None),
            P("dp", None),
            P("dp", "ctx", None),
            P(("dp", "ctx"), None),
            P(("dp", "ctx")),
            P(("dp", "ctx")),
            P(("dp", "ctx"), None),
            P(("dp", "ctx")),
            P(("dp", "ctx")),
            P(("dp", "ctx")),
            P(("dp", "ctx"), None),
            P(("dp", "ctx")),
            P(("dp", "ctx"), None),
            P(("dp", "ctx")),
            P(("dp", "ctx")),
            P(("dp", "ctx")),
            P(("dp", "ctx"), None),
            P(),
            P(),
            P(),
            P(),
            P(),
            P(),
        ),
        check_vma=False,
    )
```

```python
from functools import partial

import jax
import jax.numpy as jnp
from jax import lax
from jax.experimental import pallas as pl
from jax.experimental.pallas import tpu as pltpu
from jax.sharding import PartitionSpec as P

H = 12
HD = 64
RED = 128
PH = 2
CLS = 14


negative = -1e30
epsilon = 1e-06
highest = lax.Precision.HIGHEST


def send_rows(value, axis):
    size = lax.axis_size(axis)
    me = lax.axis_index(axis)
    came = []
    for step in range(1, size):
        sent = lax.dynamic_index_in_dim(value, (me + step) % size, 0, keepdims=False)
        came.append(lax.ppermute(sent, axis, [(k, (k + step) % size) for k in range(size)]))
    return came


def place_rows(value, came, axis):
    size = lax.axis_size(axis)
    me = lax.axis_index(axis)
    for step, row in enumerate(came, 1):
        value = lax.dynamic_update_index_in_dim(value, row, (me - step) % size, 0)
    return value


def exchange(value, axis):
    return place_rows(value, send_rows(value, axis), axis)


def summed_everywhere(value):
    for axis in ("dp", "ctx"):
        size = lax.axis_size(axis)
        step = 1
        while step < size:
            value = value + lax.ppermute(value, axis, [(k, k ^ step) for k in range(size)])
            step *= 2
    return value


def device_bits():
    bits = []
    for axis in ("dp", "ctx"):
        size = lax.axis_size(axis)
        stride = size // 2
        while stride:
            bits.append((axis, stride, size))
            stride //= 2
    return bits


def bit_orders(bits, count):
    partner = ("dp", 1, lax.axis_size("dp"))
    others = [k for k, bit in enumerate(bits) if bit != partner]
    orders = []
    for turn in range(count):
        cut = (len(others) - turn) % len(others)
        orders.append(others[cut:] + others[:cut] + [bits.index(partner)])
    return orders


def my_bit(bit):
    axis, stride, _ = bit
    return (lax.axis_index(axis) // stride) % 2


def swap(value, bit):
    axis, stride, size = bit
    return lax.ppermute(value, axis, [(k, k ^ stride) for k in range(size)])


def everyone(chunks, held):
    bits = device_bits()
    orders = bit_orders(bits, len(chunks))
    parts = list(chunks)
    for turn in range(len(bits)):
        for k, order in enumerate(orders):
            bit = bits[order[turn]]
            mine, other = parts[k], swap(parts[k], bit)
            low = my_bit(bit) == 0
            parts[k] = jnp.where(low, jnp.stack([mine, other]), jnp.stack([other, mine]))
        if turn == len(bits) - 3:
            held, parts = lax.optimization_barrier((held, parts))
    whole = []
    for part, order, chunk in zip(parts, orders, chunks):
        placed = order[::-1]
        axes = [placed.index(k) for k in range(len(bits))]
        whole.append(
            jnp.transpose(part, axes + [len(bits), len(bits) + 1]).reshape(-1, chunk.shape[1])
        )
    return whole, held


def to_owners(chunks, arriving):
    bits = device_bits()
    orders = [order[::-1] for order in bit_orders(bits, len(chunks))]
    devices = 2 ** len(bits)
    parts = [
        chunk.reshape([2] * len(bits) + [chunk.shape[0] // devices, chunk.shape[1]])
        for chunk in chunks
    ]
    left = [list(range(len(bits))) for _ in chunks]
    for turn in range(len(bits)):
        for k, order in enumerate(orders):
            axis = left[k].index(order[turn])
            bit = bits[order[turn]]
            side = my_bit(bit)
            sent = lax.dynamic_index_in_dim(parts[k], 1 - side, axis, keepdims=False)
            kept = lax.dynamic_index_in_dim(parts[k], side, axis, keepdims=False)
            came = swap(sent, bit)
            total = kept.astype(jnp.float32) + came.astype(jnp.float32)
            parts[k] = total if turn == len(bits) - 1 else total.astype(jnp.bfloat16)
            left[k].remove(order[turn])
        if turn == 2:
            arriving, parts[0] = lax.optimization_barrier((arriving, parts[0]))
    return parts, arriving


def norm_rows(hidden, gain, shift):
    average = jnp.mean(hidden, axis=-1, keepdims=True)
    centred = hidden - average
    inv_std = lax.rsqrt(jnp.mean(centred * centred, axis=-1, keepdims=True) + epsilon)
    normed = centred * inv_std
    return (normed * gain + shift, normed, inv_std)


def norm_back(upstream, normed, inv_std, gain):
    scaled = upstream * gain
    first_mean = jnp.mean(scaled, axis=-1, keepdims=True)
    second = jnp.mean(scaled * normed, axis=-1, keepdims=True)
    return inv_std * (scaled - first_mean - normed * second)


def rows_product(left, right, precision=None):
    return lax.dot_general(
        left,
        right,
        (((0,), (0,)), ((), ())),
        precision=precision,
        preferred_element_type=jnp.float32,
    )


def right_transposed(left, right, precision=None):
    return lax.dot_general(
        left,
        right,
        (((1,), (1,)), ((), ())),
        precision=precision,
        preferred_element_type=jnp.float32,
    )


def fill_bias(starts_ref, lengths_ref, bias_ref):
    regions, region, _ = bias_ref.shape
    for r in range(regions):
        key = lax.broadcasted_iota(jnp.int32, (region, region), 0)
        query = lax.broadcasted_iota(jnp.int32, (region, region), 1)
        low = starts_ref[0, r] - r * region
        high = low + lengths_ref[0, r]
        together = (key >= low) & (key < high) & (query >= low) & (query < high)
        bias_ref[r] = jnp.where((key <= query) | together, 0.0, negative)


def head_lanes(block, head):
    lane = lax.broadcasted_iota(jnp.int32, block.shape, 1)
    return jnp.where(lane // HD == head, block, jnp.zeros_like(block))


def plain_dot(left, right):
    return jnp.dot(left, right, preferred_element_type=jnp.float32)


def attention_kernel(
    starts_ref, lengths_ref, query_ref, key_ref, value_ref, mixed_ref, total_ref, bias_ref, *, span
):
    @pl.when(pl.program_id(0) == 0)
    def _():
        fill_bias(starts_ref, lengths_ref, bias_ref)

    length, lanes = query_ref.shape
    region = bias_ref.shape[1]
    queries_t = (query_ref[...] * 0.125).T
    values_t = value_ref[...].T
    heads = []
    for head in range(lanes // HD):
        keys = head_lanes(key_ref[...], head)
        rows = slice(head * HD, (head + 1) * HD)
        blocks = []
        for begin in range(0, length, span):
            r = begin // region
            reach = (r + 1) * region
            scores = plain_dot(keys[:reach], queries_t[:, begin : begin + span])
            inner = begin - r * region
            last = scores[reach - region :] + bias_ref[r, :, inner : inner + span]
            scores = jnp.concatenate([scores[: reach - region], last]) if r else last
            top = jnp.max(scores, axis=0, keepdims=True)
            weights = jnp.exp(scores - top)
            total = jnp.sum(weights, axis=0, keepdims=True)
            mixed_t = plain_dot(values_t[rows, :reach], weights.astype(jnp.bfloat16))
            blocks.append(mixed_t * (1.0 / total))
            total_ref[0, head : head + 1, begin : begin + span] = top + jnp.log(total)
        heads.append(jnp.concatenate(blocks, axis=1))
    mixed_ref[...] = jnp.concatenate(heads, axis=0).astype(jnp.bfloat16).T


def attention_back_kernel(
    starts_ref,
    lengths_ref,
    query_ref,
    key_ref,
    value_ref,
    total_ref,
    mixed_ref,
    upstream_ref,
    query_grad_ref,
    key_grad_ref,
    value_grad_ref,
    query_sum_ref,
    value_sum_ref,
    bias_ref,
    *,
    span,
):
    @pl.when(pl.program_id(0) == 0)
    def _():
        fill_bias(starts_ref, lengths_ref, bias_ref)

    length, lanes = query_ref.shape
    region = bias_ref.shape[1]
    queries = query_ref[...] * 0.125
    queries_t = queries.T
    keys_t = key_ref[...].T
    upstream = upstream_ref[...]
    upstream_t = upstream.T
    products = (upstream_t.astype(jnp.float32) * mixed_ref[...].T.astype(jnp.float32))
    query_heads = []
    key_grad = None
    value_grad = None
    lane = lax.broadcasted_iota(jnp.int32, (length, lanes), 1)
    for head in range(lanes // HD):
        keys = head_lanes(key_ref[...], head)
        values = head_lanes(value_ref[...], head)
        rows = slice(head * HD, (head + 1) * HD)
        centre = jnp.sum(products[rows], axis=0, keepdims=True)
        key_parts = [None] * (length // region)
        value_parts = [None] * (length // region)
        blocks = []
        for begin in range(0, length, span):
            r = begin // region
            reach = (r + 1) * region
            here = slice(begin, begin + span)
            scores = plain_dot(keys[:reach], queries_t[:, here])
            inner = begin - r * region
            last = scores[reach - region :] + bias_ref[r, :, inner : inner + span]
            scores = jnp.concatenate([scores[: reach - region], last]) if r else last
            probs = jnp.exp(scores - total_ref[0, head : head + 1, here])
            grad_probs = plain_dot(values[:reach], upstream_t[:, here])
            grad_scores = (probs * (grad_probs - centre[:, here])).astype(jnp.bfloat16)
            probs_low = probs.astype(jnp.bfloat16)
            value_term = plain_dot(probs_low, upstream[here])
            key_term = plain_dot(grad_scores, queries[here])
            for k in range(r + 1):
                part = slice(k * region, (k + 1) * region)
                first = key_parts[k] is None
                key_parts[k] = key_term[part] if first else key_parts[k] + key_term[part]
                value_parts[k] = value_term[part] if first else value_parts[k] + value_term[part]
            blocks.append(plain_dot(keys_t[rows, :reach], grad_scores))
        query_heads.append(jnp.concatenate(blocks, axis=1))
        key_head = jnp.concatenate(key_parts, axis=0)
        value_head = jnp.concatenate(value_parts, axis=0)
        mine = lane // HD == head
        key_grad = key_head if head == 0 else jnp.where(mine, key_head, key_grad)
        value_grad = value_head if head == 0 else jnp.where(mine, value_head, value_grad)
    query_low = (jnp.concatenate(query_heads, axis=0) * 0.125).astype(jnp.bfloat16).T
    value_low = value_grad.astype(jnp.bfloat16)
    query_grad_ref[...] = query_low
    key_grad_ref[...] = key_grad.astype(jnp.bfloat16)
    value_grad_ref[...] = value_low
    query_sum_ref[0] = jnp.sum(query_low.astype(jnp.float32), axis=0, keepdims=True)
    value_sum_ref[0] = jnp.sum(value_low.astype(jnp.float32), axis=0, keepdims=True)


def attention_specs(length, regions):
    column = pl.BlockSpec((length, 2 * HD), lambda i: (0, i))
    totals = pl.BlockSpec((1, 2, length), lambda i: (i, 0, 0))
    sums = pl.BlockSpec((1, 1, 2 * HD), lambda i: (i, 0, 0))
    scalars = pl.BlockSpec(memory_space=pltpu.SMEM)
    bias = pltpu.VMEM((regions, length // regions, length // regions), jnp.float32)
    return column, totals, sums, scalars, bias


def attention(queries, keys, values, starts, lengths):
    length, width = queries.shape
    regions = starts.shape[1]
    column, totals, sums, scalars, bias = attention_specs(length, regions)
    return pl.pallas_call(
        partial(attention_kernel, span=length // regions),
        grid=(H // 2,),
        in_specs=[scalars, scalars, column, column, column],
        out_specs=[column, totals],
        out_shape=[
            jax.ShapeDtypeStruct((length, width), jnp.bfloat16),
            jax.ShapeDtypeStruct((H // 2, 2, length), jnp.float32),
        ],
        scratch_shapes=[bias],
        name="attention",
    )(starts, lengths, queries, keys, values)


def attention_back(queries, keys, values, starts, lengths, log_total, mixed, upstream):
    length, width = queries.shape
    regions = starts.shape[1]
    column, totals, sums, scalars, bias = attention_specs(length, regions)
    grad = jax.ShapeDtypeStruct((length, width), jnp.bfloat16)
    grad_sum = jax.ShapeDtypeStruct((H // 2, 1, 2 * HD), jnp.float32)
    return pl.pallas_call(
        partial(attention_back_kernel, span=length // regions),
        grid=(H // 2,),
        in_specs=[scalars, scalars, column, column, column, totals, column, column],
        out_specs=[column, column, column, sums, sums],
        out_shape=[grad, grad, grad, grad_sum, grad_sum],
        scratch_shapes=[bias],
        name="attention_back",
    )(starts, lengths, queries, keys, values, log_total, mixed, upstream)


def gelu_kernel(first_ref, weight_ref, bias_ref, active_ref, slope_ref):
    inner = plain_dot(first_ref[...], weight_ref[...]) + bias_ref[...]
    half = 0.5 * lax.erf(inner * 0.7071067811865476) + 0.5
    active_ref[...] = (inner * half).astype(jnp.bfloat16)
    bell = jnp.exp(inner * inner * -0.5) * 0.3989422804014327
    slope_ref[...] = half + inner * bell


def gelu_forward(first_low, in_full, in_bias):
    length, width = first_low.shape
    hidden_units = in_full.shape[1]
    span = hidden_units // 6
    column = pl.BlockSpec((length, span), lambda j: (0, j))
    return pl.pallas_call(
        gelu_kernel,
        grid=(hidden_units // span,),
        in_specs=[
            pl.BlockSpec((length, width), lambda j: (0, 0)),
            pl.BlockSpec((width, span), lambda j: (0, j)),
            pl.BlockSpec((1, span), lambda j: (0, j)),
        ],
        out_specs=[column, column],
        out_shape=[
            jax.ShapeDtypeStruct((length, hidden_units), jnp.bfloat16),
            jax.ShapeDtypeStruct((length, hidden_units), jnp.float32),
        ],
        name="gelu_forward",
    )(first_low, in_full, in_bias[None])


def gelu_back_kernel(upstream_ref, weight_ref, slope_ref, grad_ref, sum_ref):
    grad = right_transposed(upstream_ref[...], weight_ref[...]) * slope_ref[...]
    low = grad.astype(jnp.bfloat16)
    grad_ref[...] = low
    sum_ref[...] = jnp.sum(low.astype(jnp.float32), axis=0, keepdims=True)


def gelu_backward(upstream, back_full, slope):
    length, width = upstream.shape
    hidden_units = back_full.shape[0]
    span = hidden_units // 6
    column = pl.BlockSpec((length, span), lambda j: (0, j))
    return pl.pallas_call(
        gelu_back_kernel,
        grid=(hidden_units // span,),
        in_specs=[
            pl.BlockSpec((length, width), lambda j: (0, 0)),
            pl.BlockSpec((span, width), lambda j: (j, 0)),
            column,
        ],
        out_specs=[column, pl.BlockSpec((1, span), lambda j: (0, j))],
        out_shape=[
            jax.ShapeDtypeStruct((length, hidden_units), jnp.bfloat16),
            jax.ShapeDtypeStruct((1, hidden_units), jnp.float32),
        ],
        name="gelu_backward",
    )(upstream, back_full, slope)


def interleave(rows, devices):
    width = rows.shape[1]
    part = rows.shape[0] // (4 * devices)
    split = rows.reshape(devices, 4, part, width)
    return jnp.swapaxes(split, 1, 2).reshape(devices * part, 4 * width)


def separate(columns, devices):
    width = columns.shape[1] // 4
    part = columns.shape[0] // devices
    split = columns.reshape(devices, part, 4, width)
    return jnp.swapaxes(split, 1, 2).reshape(devices * 4 * part, width)


def vector_columns(vectors, hidden_vector, devices):
    columns = [vector[:, None] for vector in vectors]
    columns.append(interleave(hidden_vector[:, None], devices))
    packed = jnp.concatenate(columns, axis=1)
    return jnp.pad(packed, ((0, 0), (0, 128 - packed.shape[1])))


def shards(
    tokens,
    out_grad,
    logit_grad,
    piece_start,
    piece_len,
    qkv_weight,
    query_bias,
    value_bias,
    out_weight,
    out_bias,
    gain_one,
    shift_one,
    in_weight,
    in_bias,
    back_weight,
    back_bias,
    gain_two,
    shift_two,
    reduce_weight,
    reduce_bias,
    pool_query,
    pool_weight,
    pool_bias,
    class_weight,
    class_bias,
):
    seq_count, local_len, width = tokens.shape
    ctx_size = lax.axis_size("ctx")
    assert seq_count == ctx_size
    devices = lax.axis_size("dp") * ctx_size
    hidden_units = in_weight.shape[1]
    assert hidden_units == 4 * width
    full_len = local_len * ctx_size
    head_width = RED // PH
    mine = lax.axis_index("ctx")
    query_rows = pool_query.astype(jnp.float32).reshape(PH, head_width)
    pool_weight_f = pool_weight.astype(jnp.float32)
    class_weight_f = class_weight.astype(jnp.float32)
    reduce_shift = reduce_bias.astype(jnp.float32)
    pool_shift = pool_bias.astype(jnp.float32)
    class_shift = class_bias.astype(jnp.float32)
    starts = lax.dynamic_slice_in_dim(piece_start, mine, 1, 0)
    lengths = lax.dynamic_slice_in_dim(piece_len, mine, 1, 0)
    logit_row = lax.dynamic_slice_in_dim(logit_grad, mine, 1, 0)

    small = vector_columns(
        (query_bias, value_bias, out_bias, gain_one, shift_one, back_bias, gain_two, shift_two),
        in_bias,
        1,
    )
    half = width // 2
    part = in_weight.shape[0]
    late = jnp.concatenate(
        [in_weight[:, k * width : (k + 1) * width] for k in range(4)] + [back_weight], axis=0
    )
    seq_tokens = exchange(tokens, "ctx").reshape(full_len, width)
    early, late = everyone(
        [
            jnp.concatenate([qkv_weight[:, :width], small, reduce_weight], axis=1),
            jnp.concatenate([qkv_weight[:, width : 2 * width], out_weight[:, :half]], axis=1),
            jnp.concatenate([qkv_weight[:, 2 * width :], out_weight[:, half:]], axis=1),
        ],
        late,
    )
    late = lax.all_gather(late, ("dp", "ctx"), axis=0)
    query_weight = early[0][:, :width]
    key_weight = early[1][:, :width]
    value_weight = early[2][:, :width]
    out_full = jnp.concatenate([early[1][:, width:], early[2][:, width:]], axis=1)
    reduce_full = early[0][:, width + 128 :]
    vectors = early[0][:, width : width + 128].astype(jnp.float32)
    q_bias, v_bias, o_bias, g_one, s_one, b_bias, g_two, s_two = [vectors[:, k] for k in range(8)]
    i_bias = separate(vectors[:, 8:12], devices)[:, 0]
    in_full = jnp.concatenate(
        [late[:, k * part : (k + 1) * part].reshape(width, width) for k in range(4)], axis=1
    )
    back_full = late[:, 4 * part :].reshape(hidden_units, width)

    def project(weight):
        return jnp.dot(seq_tokens, weight, preferred_element_type=jnp.float32)

    queries = (project(query_weight) + q_bias).astype(jnp.bfloat16)
    keys = project(key_weight).astype(jnp.bfloat16)
    values = (project(value_weight) + v_bias).astype(jnp.bfloat16)
    out_grad, queries = lax.optimization_barrier((out_grad, queries))
    seq_out_grad = exchange(out_grad, "ctx").reshape(full_len, width)
    mixed_low, log_total = attention(queries, keys, values, starts, lengths)
    attended = jnp.dot(mixed_low, out_full, preferred_element_type=jnp.float32) + o_bias
    first_norm, normed_one, inv_one = norm_rows(
        seq_tokens.astype(jnp.float32) + attended, g_one, s_one
    )
    first_low = first_norm.astype(jnp.bfloat16)
    active_low, slope = gelu_forward(first_low, in_full, i_bias)
    branch = jnp.dot(active_low, back_full, preferred_element_type=jnp.float32) + b_bias
    result, normed_two, inv_two = norm_rows(first_norm + branch, g_two, s_two)
    result_low = result.astype(jnp.bfloat16)
    layer_out = exchange(result_low.reshape(ctx_size, local_len, width), "ctx")
    reduced = jnp.dot(result_low, reduce_full, preferred_element_type=jnp.float32) + reduce_shift
    pool_heads = reduced.reshape(full_len, PH, head_width)
    pool_scores = jnp.einsum("lpe,pe->lp", pool_heads, query_rows, precision=highest) * 0.125
    pool_top = jnp.max(pool_scores, axis=0)
    pool_exp = jnp.exp(pool_scores - pool_top)
    pool_total = jnp.sum(pool_exp, axis=0)
    pool_probs = pool_exp / pool_total
    pooled_heads = jnp.einsum("lp,lpe->pe", pool_probs, pool_heads, precision=highest)
    pooled = pooled_heads.reshape(1, RED)
    hidden = jnp.tanh(jnp.dot(pooled, pool_weight_f, precision=highest) + pool_shift)
    logit_mine = jnp.dot(hidden, class_weight_f, precision=highest) + class_shift
    logits = exchange(jnp.broadcast_to(logit_mine[None], (ctx_size, 1, CLS)), "ctx")[:, 0]

    grad_class = rows_product(hidden, logit_row, highest)
    grad_class_bias = jnp.sum(logit_row, axis=0)
    grad_hidden = right_transposed(logit_row, class_weight_f, highest)
    grad_pre = grad_hidden * (1.0 - hidden * hidden)
    grad_pool_weight = rows_product(pooled, grad_pre, highest)
    grad_pool_bias = jnp.sum(grad_pre, axis=0)
    grad_pooled = right_transposed(grad_pre, pool_weight_f, highest).reshape(PH, head_width)
    pool_along = jnp.einsum(
        "lpe,pe->lp", pool_heads, grad_pooled, precision=highest
    ) - jnp.sum(pooled_heads * grad_pooled, axis=-1)
    grad_pool_scores = pool_probs * pool_along
    grad_reduced = (
        pool_probs[..., None] * grad_pooled + grad_pool_scores[..., None] * query_rows * 0.125
    )
    grad_query = (
        jnp.einsum("lp,lpe->pe", grad_pool_scores, pool_heads, precision=highest).reshape(RED)
        * 0.125
    )
    grad_red_low = grad_reduced.reshape(full_len, RED).astype(jnp.bfloat16)
    grad_reduce_bias = jnp.sum(grad_red_low.astype(jnp.float32), axis=0)
    tiny = summed_everywhere(
        jnp.concatenate(
            [
                grad_pool_weight,
                jnp.pad(grad_class.T, ((0, 16 - CLS), (0, 0))),
                jnp.pad(grad_class_bias, (0, RED - CLS))[None],
                grad_pool_bias[None],
                grad_query[None],
                grad_reduce_bias[None],
                jnp.zeros((4, RED), jnp.float32),
            ],
            axis=0,
        )
    )
    grad_reduce = rows_product(result_low, grad_red_low)
    grad_result = seq_out_grad.astype(jnp.float32) + right_transposed(grad_red_low, reduce_full)
    grad_gain_two = jnp.sum(grad_result * normed_two, axis=0)
    grad_shift_two = jnp.sum(grad_result, axis=0)
    grad_mid = norm_back(grad_result, normed_two, inv_two, g_two)
    grad_branch_low = grad_mid.astype(jnp.bfloat16)
    grad_back_bias = jnp.sum(grad_branch_low.astype(jnp.float32), axis=0)
    grad_back = rows_product(active_low, grad_branch_low)
    grad_inner_low, grad_in_bias = gelu_backward(grad_branch_low, back_full, slope)
    grad_in_bias = grad_in_bias[0]
    grad_in = rows_product(first_low, grad_inner_low)
    grad_in = grad_in.astype(jnp.bfloat16)
    packed = jnp.concatenate(
        [grad_in[:, k * width : (k + 1) * width].reshape(devices, part, width) for k in range(4)]
        + [grad_back.astype(jnp.bfloat16).reshape(devices, 4 * part, width)],
        axis=1,
    )
    packed, grad_inner_low = lax.optimization_barrier((packed, grad_inner_low))
    early_owned = lax.psum_scatter(
        packed.reshape(devices * 8 * part, width), ("dp", "ctx"), scatter_dimension=0, tiled=True
    ).astype(jnp.float32)
    grad_first = grad_mid + right_transposed(grad_inner_low, in_full)
    grad_gain_one = jnp.sum(grad_first * normed_one, axis=0)
    grad_shift_one = jnp.sum(grad_first, axis=0)
    grad_start = norm_back(grad_first, normed_one, inv_one, g_one)
    grad_attn_low = grad_start.astype(jnp.bfloat16)
    grad_out_bias = jnp.sum(grad_attn_low.astype(jnp.float32), axis=0)
    (tiny, layer_out, logits), grad_attn_low = lax.optimization_barrier(
        ((tiny, layer_out, logits), grad_attn_low)
    )
    grad_out = rows_product(mixed_low, grad_attn_low)
    grad_mixed_low = right_transposed(grad_attn_low, out_full).astype(jnp.bfloat16)
    query_grad, key_grad, value_grad, query_sum, value_sum = attention_back(
        queries, keys, values, starts, lengths, log_total, mixed_low, grad_mixed_low
    )
    grad_query_bias = query_sum.reshape(width)
    grad_value_bias = value_sum.reshape(width)
    grad_small = vector_columns(
        (
            grad_query_bias,
            grad_value_bias,
            grad_out_bias,
            grad_gain_one,
            grad_shift_one,
            grad_back_bias,
            grad_gain_two,
            grad_shift_two,
        ),
        grad_in_bias,
        devices,
    )
    grad_out = grad_out.astype(jnp.bfloat16)

    def weight_grad(upstream):
        return rows_product(seq_tokens, upstream).astype(jnp.bfloat16)

    token_grad = (
        grad_start
        + right_transposed(query_grad, query_weight)
        + right_transposed(key_grad, key_weight)
        + right_transposed(value_grad, value_weight)
    ).astype(jnp.bfloat16)
    token_rows = token_grad.reshape(ctx_size, local_len, width)
    arriving = send_rows(token_rows, "ctx")
    late_owned, arriving = to_owners(
        [
            jnp.concatenate(
                [
                    weight_grad(query_grad),
                    grad_small.astype(jnp.bfloat16),
                    grad_reduce.astype(jnp.bfloat16),
                ],
                axis=1,
            ),
            jnp.concatenate([weight_grad(key_grad), grad_out[:, :half]], axis=1),
            jnp.concatenate([weight_grad(value_grad), grad_out[:, half:]], axis=1),
        ],
        arriving,
    )
    token_grad = place_rows(token_rows, arriving, "ctx")
    small_owned = late_owned[0][:, width : width + 128]
    tall = RED + 16
    return (
        layer_out,
        logits,
        token_grad,
        jnp.concatenate([owned[:, :width] for owned in late_owned], axis=1),
        small_owned[:, 0],
        small_owned[:, 1],
        jnp.concatenate([late_owned[1][:, width:], late_owned[2][:, width:]], axis=1),
        small_owned[:, 2],
        small_owned[:, 3],
        small_owned[:, 4],
        jnp.concatenate([early_owned[k * part : (k + 1) * part] for k in range(4)], axis=1),
        separate(small_owned[:, 8:12], 1)[:, 0],
        early_owned[4 * part :],
        small_owned[:, 5],
        small_owned[:, 6],
        small_owned[:, 7],
        late_owned[0][:, width + 128 :],
        tiny[tall + 3],
        tiny[tall + 2],
        tiny[:RED],
        tiny[tall + 1],
        tiny[RED : RED + CLS].T,
        tiny[tall, :CLS],
    )


def solution(mesh):
    placed = (
        P("dp", "ctx", None),
        P("dp", "ctx", None),
        P("dp", None),
        P("dp", None),
        P("dp", None),
        P(("dp", "ctx"), None),
        P(("dp", "ctx")),
        P(("dp", "ctx")),
        P(("dp", "ctx"), None),
        P(("dp", "ctx")),
        P(("dp", "ctx")),
        P(("dp", "ctx")),
        P(("dp", "ctx"), None),
        P(("dp", "ctx")),
        P(("dp", "ctx"), None),
        P(("dp", "ctx")),
        P(("dp", "ctx")),
        P(("dp", "ctx")),
        P(("dp", "ctx"), None),
        P(),
        P(),
        P(),
        P(),
        P(),
        P(),
    )
    return jax.shard_map(
        shards,
        mesh=mesh,
        in_specs=placed,
        out_specs=(
            P("dp", "ctx", None),
            P("dp", None),
            P("dp", "ctx", None),
            P(("dp", "ctx"), None),
            P(("dp", "ctx")),
            P(("dp", "ctx")),
            P(("dp", "ctx"), None),
            P(("dp", "ctx")),
            P(("dp", "ctx")),
            P(("dp", "ctx")),
            P(("dp", "ctx"), None),
            P(("dp", "ctx")),
            P(("dp", "ctx"), None),
            P(("dp", "ctx")),
            P(("dp", "ctx")),
            P(("dp", "ctx")),
            P(("dp", "ctx"), None),
            P(),
            P(),
            P(),
            P(),
            P(),
            P(),
        ),
        check_vma=False,
    )
```
